32 devices in a mesh: groups: 2 (over x), rows: 8 (over z, y), bands: 2 (over core).
Axes of the slice: x: 2, y: 2, z: 4, core: 2. Of those that a mesh axis runs over, the one named last changes fastest.
Arguments:
- radiance: bfloat16 [224, 512, 1024], P('bands', ('groups', 'rows')), parts along dimension 1, may hold values from -6 to 6
- response: bfloat16 [224], P('bands'), may hold values from 0.019897461 to 0.19921875
- reference_tiles: float32 [32, 128, 128], P(('groups', 'rows')), parts along dimension 0, may hold values from -6 to 6
- chip_owner: int32 [60, 1], P('groups'), parts along dimension 0, may hold values from 0 to 7; in each aligned block of 15 rows (0 to 14, 15 to 29, ...) at most 2 rows name the same one
- tile_slot: int32 [60], P('groups'), parts along dimension 0, may hold values from 0 to 1
- row_offset: int32 [60], P('groups'), parts along dimension 0, may hold values from -127 to 127
- column_offset: int32 [60], P('groups'), parts along dimension 0, may hold values from -512 to 511
- valid_rows: int32 [2], P('groups'), parts along dimension 0, may hold values from 128 to 256
Outputs:
- aligned: bfloat16 [224, 512, 1024], P('bands', ('groups', 'rows')), parts along dimension 1
- surface: float32 [512, 1920], P(('groups', 'rows')), parts along dimension 0
The draws below stay inside these ranges and needn't reach their ends.
There are 2 independent parts, one for each index of `groups`. The reference program is written for one: setup_inputs(seed, part) draws one part's arguments, and reference() takes and returns one part's arrays. A program takes and returns all parts, laid end to end along the dimension named above; an argument that names none is the same for every part. Nothing has to cross between parts.
Inputs may be any that keep to these rules, and one draw needn't show every extreme that they name: `chip_owner`: among the 15 chips of one chip row (chips k * 15 to k * 15 + 14) no owner is named more than 2 times, and in some chip row one owner is named exactly 2 times; every owner is named by some chip.
All inputs are finite; a program needn't handle non-finite values.
Results may differ from the reference program's by a relative error of at most 0.011.
Values may be sent and summed in bfloat16 or wider, within the bound.
A program may use at most 128 MiB of HBM per device.

```python
import math
import jax
import jax.numpy as jnp
import numpy as np
from jax import lax

BANDS = 224
WIDTH = 1024
CHIP = 128
TILE_DEV = 2
MAXDY = 2
ROWS = 256
ACROSS = 15
MOST = 2
CHIP_ROWS = 2
NCHIP = 30
TILES = 16
OWNERS = 8


def draw_row_offset(key, part):
    sign_key = jax.random.fold_in(key, 11)
    size_key = jax.random.fold_in(key, 12)
    jitter_key = jax.random.fold_in(key, 13)
    signs = 2 * jax.random.randint(sign_key, (CHIP_ROWS,), 0, 2) - 1
    common = signs * jax.random.randint(size_key, (CHIP_ROWS,), MAXDY * 48, MAXDY * 60 + 1)
    jitter = jax.random.randint(jitter_key, (CHIP_ROWS, ACROSS), -7, 8)
    return (common[:, None] + jitter).reshape(NCHIP).astype(jnp.int32)


def set_ends(values, key, low, high):
    longest = values.shape.index(max(values.shape))
    spots = []
    for shift in (0, 1):
        where = [jax.random.randint(jax.random.fold_in(key, axis), (), 0, length) for axis, length in enumerate(values.shape)]
        where[longest] = (where[longest] + shift) % values.shape[longest]
        spots.append(tuple(where))
    return values.at[spots[0]].set(low).at[spots[1]].set(high)


def shard_levels(stream_key, shape, pieces, least, largest):
    def one(dim, shards_of):
        heights = jax.random.uniform(jax.random.fold_in(jax.random.fold_in(stream_key, 6), dim), (shards_of,), jnp.float32, least / len(pieces), largest / len(pieces))
        return jnp.repeat(jnp.exp(heights), shape[dim] // shards_of).reshape((-1,) + (1,) * (len(shape) - dim - 1))

    level = one(*pieces[0])
    for cut in pieces[1:]:
        level = level * one(*cut)
    return level


def shared_out(key, own, number, rows, number_of, top, bound, slope):
    sequence = jax.random.permutation(key, number_of)
    packed, ordinary = shares(number_of, rows * top, bound, slope, True), shares(number_of, rows * top, bound, slope, False)
    places = jnp.arange(number_of)

    def named(tallies, offset_by):
        used = int((tallies > 0).sum())
        fixed = max(1, used // 4)
        moved = fixed + (places - fixed + offset_by * (used - fixed)) % max(1, number_of - fixed)
        return jnp.zeros((number_of,), jnp.int32).at[sequence[jnp.where(places < fixed, places, moved)]].set(jnp.asarray(tallies, jnp.int32))

    tallies = jnp.where(number % 4 == 0, named(packed, number // 4), named(ordinary, number - number // 4 - 1))
    mixed = jax.random.permutation(jax.random.fold_in(own, 3), number_of)
    source_of, receiver = mixed[0:number_of // 2 * 2:2], mixed[1:number_of // 2 * 2:2]
    room = jnp.minimum(tallies[source_of] - 1, bound - tallies[receiver]) // 2
    room = jnp.where((source_of == sequence[0]) | (receiver == sequence[0]) | (tallies[receiver] == 0), 0, jnp.maximum(room, 0))
    moved = jax.random.randint(jax.random.fold_in(own, 4), (number_of // 2,), 0, 1 << 20) % (room + 1)
    tallies = tallies.at[source_of].add(-moved).at[receiver].add(moved)
    items = jnp.searchsorted(jnp.cumsum(tallies), jnp.arange(rows * top), side="right").astype(jnp.int32)
    listing = items.reshape(top, rows).T
    listing = listing[jax.random.permutation(jax.random.fold_in(own, 1), rows)]
    offset_by = jax.random.randint(jax.random.fold_in(own, 2), (rows, 1), 0, top)
    return jnp.take_along_axis(listing, (jnp.arange(top)[None, :] + offset_by) % top, axis=1)


def shares(amount, total, bound, skew, full):
    weights = [(1 << 20) // math.isqrt(grade ** skew) + 1 for grade in range(1, amount + 1)]
    largest = bound if full else min(bound, max(-(-total // amount), total * weights[0] // sum(weights)))
    least = 1 if total - largest >= amount - 1 else 0
    counts, surplus = [largest] + [least] * (amount - 1), total - largest - least * (amount - 1)
    while surplus > 0:
        candidates = [i for i in range(1, amount) if counts[i] < largest] or [i for i in range(1, amount) if counts[i] < bound]
        pool, remaining = sum([weights[i] for i in candidates]), surplus
        for i in candidates:
            addition = min(bound - counts[i], max(1, remaining * weights[i] // pool), surplus)
            counts[i] = counts[i] + addition
            surplus = surplus - addition
    return np.array(counts)


def normal_values(stream_key, extent, spread, most, shards=(), kind=jnp.bfloat16):
    values = jax.random.normal(stream_key, extent, jnp.float32) * spread
    if len(shards) > 0:
        values = shard_levels(stream_key, extent, shards, -0.22, 0.18) * values
    return jnp.clip(values, min=-most, max=most).astype(kind)


def setup_inputs(seed: int = 0, part: int = 0) -> dict:
    arg_keys = jax.random.split(jax.random.key(seed), 9)
    part_splits = jax.random.split(jax.random.fold_in(arg_keys[8], part), 9)
    radiance = normal_values(part_splits[0], (BANDS, ROWS, WIDTH), 1.0, 6.0, ((0, 2), (1, 8)))
    response = jnp.clip(jnp.exp(math.log(0.19921875) - 2.3038113 * jax.random.uniform(arg_keys[1], (BANDS,), jnp.float32) ** shard_levels(arg_keys[1], (BANDS,), ((0, 2),), -0.2, 0.2)), 0.019897461, 0.19921875).astype(jnp.bfloat16)
    reference_tiles = normal_values(part_splits[2], (TILES, CHIP, CHIP), 1.0, 6.0, ((0, 8),), jnp.float32)
    chip_owner_keys = jax.random.split(jax.random.fold_in(part_splits[3], 1), NCHIP // ACROSS)
    chip_owner_turns = jax.random.permutation(jax.random.fold_in(part_splits[3], 3), NCHIP // ACROSS)
    chip_owner = jax.vmap(lambda own, number: shared_out(jax.random.fold_in(part_splits[3], 2), own, number, ACROSS, OWNERS, 1, MOST, 2))(chip_owner_keys, chip_owner_turns).reshape((NCHIP, 1))
    tile_slot = set_ends(jax.random.randint(part_splits[4], (NCHIP,), 0, TILE_DEV), jax.random.fold_in(part_splits[4], 1), 0, TILE_DEV - 1).astype(jnp.int32)
    row_offset = draw_row_offset(jax.random.fold_in(jax.random.fold_in(arg_keys[8], part), 71), part)
    column_offset = set_ends(jax.random.randint(part_splits[6], (NCHIP,), -512, 512), jax.random.fold_in(part_splits[6], 1), -512, 511).astype(jnp.int32)
    valid_rows = jax.random.randint(part_splits[7], (1,), ROWS // 2, ROWS + 1).astype(jnp.int32)
    return dict(radiance=radiance, response=response, reference_tiles=reference_tiles, chip_owner=chip_owner, tile_slot=tile_slot, row_offset=row_offset, column_offset=column_offset, valid_rows=valid_rows)


highest = lax.Precision.HIGHEST


def hann_at(positions, length):
    return 0.5 - 0.5 * jnp.cos(positions * (2.0 * math.pi / length))


def chip_tables(length):
    indices = jnp.arange(length, dtype=jnp.int32)
    angles = (jnp.outer(indices, indices) % length).astype(jnp.float32) * (2.0 * math.pi / length)
    return jnp.cos(angles), jnp.sin(angles)


def forward_spectra(blocks, cosine_table, sine_table):
    column_real = jnp.einsum("npq,qv->npv", blocks, cosine_table, precision=highest)
    column_imag = -jnp.einsum("npq,qv->npv", blocks, sine_table, precision=highest)
    spec_real = jnp.einsum("up,npv->nuv", cosine_table, column_real, precision=highest) + jnp.einsum("up,npv->nuv", sine_table, column_imag, precision=highest)
    spec_imag = jnp.einsum("up,npv->nuv", cosine_table, column_imag, precision=highest) - jnp.einsum("up,npv->nuv", sine_table, column_real, precision=highest)
    return spec_real, spec_imag


def inverse_surface(cross_real, cross_imag, cosine_table, sine_table):
    back_real = jnp.einsum("up,npv->nuv", cosine_table, cross_real, precision=highest) - jnp.einsum("up,npv->nuv", sine_table, cross_imag, precision=highest)
    back_imag = jnp.einsum("up,npv->nuv", cosine_table, cross_imag, precision=highest) + jnp.einsum("up,npv->nuv", sine_table, cross_real, precision=highest)
    result = jnp.einsum("nuq,qv->nuv", back_real, cosine_table, precision=highest) - jnp.einsum("nuq,qv->nuv", back_imag, sine_table, precision=highest)
    return result / float(CHIP) ** 3


def keys_kernel(distance):
    magnitude = jnp.abs(distance)
    inner_part = (1.5 * magnitude - 2.5) * magnitude * magnitude + 1.0
    outer_part = ((-0.5 * magnitude + 2.5) * magnitude - 4.0) * magnitude + 2.0
    return jnp.where(magnitude <= 1.0, inner_part, jnp.where(magnitude < 2.0, outer_part, 0.0))


def offset_fields(row_offset, column_offset, across, first_row, row_count):
    chip_rows = row_offset.shape[0] // across
    stacked = jnp.stack([row_offset, column_offset], axis=1).astype(jnp.float32)
    row_means = jnp.sum(stacked.reshape(chip_rows, across, 2), axis=1) / (64.0 * across)
    centres = jnp.arange(chip_rows, dtype=jnp.float32) * CHIP + (CHIP - 1) * 0.5
    positions = first_row + jnp.arange(row_count, dtype=jnp.float32)
    clipped = jnp.clip(positions, centres[0], centres[chip_rows - 1])
    weights = jnp.maximum(1.0 - jnp.abs(clipped[:, None] - centres[None, :]) / CHIP, 0.0)
    return jnp.dot(weights, row_means, precision=highest)


def shift_tables(row_width):
    half_width = row_width // 2
    samples = jnp.arange(row_width, dtype=jnp.int32)
    frequency = jnp.arange(half_width, dtype=jnp.int32)
    angles = (jnp.outer(samples, frequency) % row_width).astype(jnp.float32) * (2.0 * math.pi / row_width)
    forward = jnp.concatenate([jnp.cos(angles), jnp.sin(angles)], axis=1).astype(jnp.bfloat16)
    scaling = jnp.where(frequency == 0, 1.0, 2.0) / row_width
    inverse = jnp.concatenate([jnp.cos(angles).T * scaling[:, None], jnp.sin(angles).T * scaling[:, None]], axis=0).astype(jnp.bfloat16)
    return forward, inverse, frequency.astype(jnp.float32)


def rotate(spectrum, shifts, frequency, row_width):
    half_width = row_width // 2
    cosine_part = spectrum[..., :half_width]
    sine_part = spectrum[..., half_width:]
    angles = (2.0 * math.pi / row_width) * frequency[None, :] * shifts[:, None]
    turn_cos = jnp.cos(angles)
    turn_sin = jnp.sin(angles)
    real_part = cosine_part * turn_cos - sine_part * turn_sin
    imag_part = cosine_part * turn_sin + sine_part * turn_cos
    return jnp.concatenate([real_part, imag_part], axis=-1).astype(jnp.bfloat16)


def reference(radiance, response, reference_tiles, chip_owner, tile_slot, row_offset, column_offset, valid_rows):
    across = ACROSS
    row_numbers = jnp.arange(ROWS, dtype=jnp.int32)
    keep_rows = row_numbers < valid_rows[0]
    masked = radiance * keep_rows.astype(jnp.bfloat16)[None, :, None]
    synthetic = jnp.dot(response[None, :], masked.reshape(BANDS, ROWS * WIDTH), preferred_element_type=jnp.float32).reshape(ROWS, WIDTH)

    window = hann_at(jnp.arange(CHIP, dtype=jnp.float32), CHIP)
    window_square = window[:, None] * window[None, :]
    halves = synthetic.reshape(CHIP_ROWS, CHIP, 2 * WIDTH // CHIP, CHIP // 2)
    cells = jnp.concatenate([halves[:, :, :-1], halves[:, :, 1:]], axis=-1)
    chip_blocks = cells.transpose(0, 2, 1, 3).reshape(NCHIP, CHIP, CHIP) * window_square
    cosine_table, sine_table = chip_tables(CHIP)
    chip_real, chip_imag = forward_spectra(chip_blocks, cosine_table, sine_table)
    tile_real, tile_imag = forward_spectra(reference_tiles * window_square, cosine_table, sine_table)
    tile_index = (chip_owner[:, 0] * TILE_DEV + tile_slot).astype(jnp.int32)
    ref_real = tile_real[tile_index]
    ref_imag = tile_imag[tile_index]
    cross_real = chip_real * ref_real + chip_imag * ref_imag
    cross_imag = chip_imag * ref_real - chip_real * ref_imag
    correlation = inverse_surface(cross_real, cross_imag, cosine_table, sine_table)
    surface = correlation.reshape(CHIP_ROWS, across, CHIP, CHIP).transpose(0, 2, 1, 3).reshape(ROWS, across * CHIP)

    forward, inverse, frequency = shift_tables(WIDTH)
    fields = offset_fields(row_offset, column_offset, across, 0.0, ROWS)
    positions = jnp.arange(ROWS, dtype=jnp.float32)
    sources = positions - fields[:, 0]
    resample = keys_kernel(positions[None, :] - sources[:, None]).astype(jnp.bfloat16)
    keep_float = keep_rows.astype(jnp.float32)

    def align_band(band_plane):
        spectrum = jnp.dot(band_plane, forward, preferred_element_type=jnp.float32)
        rotated = rotate(spectrum, fields[:, 1], frequency, WIDTH)
        shifted = jnp.dot(rotated, inverse, preferred_element_type=jnp.float32).astype(jnp.bfloat16)
        resampled = jnp.dot(resample, shifted, preferred_element_type=jnp.float32)
        return (resampled * keep_float[:, None]).astype(jnp.bfloat16)

    aligned = lax.map(align_band, masked)
    return aligned, surface
```

```python
import functools
import math

import jax
import jax.numpy as jnp
import numpy as np
from jax import lax
from jax.experimental import pallas as pl
from jax.experimental.pallas import tpu as pltpu
from jax.sharding import PartitionSpec as P

CHIP = 128
MAXDY = 2
RIM = MAXDY + 1
GROUP = 16
PACK = 8

MESH = pl.DeviceIdType.MESH
bf16 = jnp.bfloat16
f32 = jnp.float32


def as_bf16(a):
    return np.asarray(a, np.float32).astype(jnp.bfloat16)


def split_np(a):
    a = np.asarray(a, np.float64)
    high = as_bf16(a)
    return high, as_bf16(a - high.astype(np.float64))


def shift_tables(width):
    half = width // 2
    samples = np.arange(half)
    tables = []
    for parity in (0, 1):
        freq = np.arange(parity, half, 2)
        angle = (np.outer(samples, freq) % width) * (2.0 * np.pi / width)
        forward = np.concatenate([np.cos(angle), np.sin(angle)], axis=1)
        scale = np.where(freq == 0, 1.0, 2.0)[:, None] / width
        inverse = np.concatenate([np.cos(angle).T * scale, np.sin(angle).T * scale], axis=0)
        tables += [as_bf16(forward), as_bf16(inverse)]
    return tables


def chip_tables():
    index = np.arange(CHIP)
    angle = (np.outer(index, index) % CHIP) * (2.0 * np.pi / CHIP)
    c, s = np.cos(angle), np.sin(angle)
    window = 0.5 - 0.5 * np.cos(index * (2.0 * np.pi / CHIP))
    columns = window[:, None] * np.concatenate([c, -s], axis=1)
    cw, sw = c * window, s * window
    rows = np.block([[cw, sw], [-sw, cw]])
    last = np.concatenate([c, -s], axis=0) / float(CHIP) ** 3
    return columns, rows, c, s, last


def dot(a, b):
    return jnp.dot(a, b, preferred_element_type=f32)


def split(a):
    high = a.astype(bf16)
    return high, (a - high.astype(f32)).astype(bf16)


def dot3(a, b):
    (ah, al), (bh, bl) = a, b
    return dot(ah, bh) + dot(ah, bl) + dot(al, bh)


def shift_rows(x, cos, sin, fe, ge, fo, go):
    rows, width = x.shape
    half, quarter = width // 2, width // 4
    period = cos.shape[0]
    lo, hi = x[:, :half], x[:, half:]

    def part(values, forward, inverse, first):
        spectrum = dot(values, forward)
        turn_c = cos[:, first : first + quarter][None]
        turn_s = sin[:, first : first + quarter][None]
        c = spectrum[:, :quarter].reshape(rows // period, period, quarter)
        s = spectrum[:, quarter:].reshape(rows // period, period, quarter)
        p = (c * turn_c - s * turn_s).reshape(rows, quarter).astype(bf16)
        q = (c * turn_s + s * turn_c).reshape(rows, quarter).astype(bf16)
        return dot(p, inverse[:quarter]) + dot(q, inverse[quarter:])

    even = part(lo + hi, fe[...], ge[...], 0)
    odd = part(lo - hi, fo[...], go[...], quarter)
    return (even + odd).astype(bf16), (even - odd).astype(bf16)


def shift_kernel(
    near,
    resp_ref, x_hbm, tiles_ref, keep_ref, cos_ref, sin_ref, fe, ge, fo, go,
    xs_hbm, syn_out, tiles_out,
    xbuf, obuf, partial, other, total, syn_buf, tile_buf,
    in_sem, out_sem, pair_sem, syn_send, syn_recv, tile_send, tile_recv,
):
    count = lax.axis_size("rows")
    me = lax.axis_index("rows")
    core = lax.axis_index("bands")
    steps, group, height, width = xbuf.shape
    in_copies = [
        pltpu.make_async_copy(x_hbm.at[pl.ds(g * group, group)], xbuf.at[g], in_sem.at[g])
        for g in range(steps)
    ]
    for copy in in_copies:
        copy.start()

    barrier = pltpu.get_barrier_semaphore()
    for d in range(1, count):
        pl.semaphore_signal(
            barrier, inc=1, device_id={"rows": lax.rem(me + d, count)}, device_id_type=MESH
        )
    pl.semaphore_signal(barrier, inc=1, device_id={"bands": 1 - core}, device_id_type=MESH)
    pl.semaphore_wait(barrier, count)

    tile_copies = []
    for d in range(1, count):
        copy = pltpu.make_async_remote_copy(
            src_ref=tiles_ref, dst_ref=tile_buf.at[d], send_sem=tile_send.at[d],
            recv_sem=tile_recv.at[d], device_id={"rows": lax.rem(me + d, count)},
            device_id_type=MESH,
        )
        copy.start()
        tile_copies.append(copy)

    acc = jnp.zeros((height, width), f32)
    for g in range(steps):
        in_copies[g].wait()

        def add(b, acc, g=g):
            return acc + resp_ref[g * group + b] * xbuf[g, b].astype(f32)

        acc = lax.fori_loop(0, group, add, acc)
    partial[...] = (acc * keep_ref[...]).astype(bf16)
    pair = pltpu.make_async_remote_copy(
        src_ref=partial, dst_ref=other, send_sem=pair_sem.at[0], recv_sem=pair_sem.at[1],
        device_id={"bands": 1 - core}, device_id_type=MESH,
    )
    pair.start()

    def out_copy(g):
        return pltpu.make_async_copy(
            obuf.at[g], xs_hbm.at[pl.ds(g * group * height, group * height)], out_sem.at[g]
        )

    def shift_step(g, carry):
        x = xbuf[g].reshape(group * height, width)
        left, right = shift_rows(x, cos_ref[...], sin_ref[...], fe, ge, fo, go)
        obuf[g, :, : width // 2] = left
        obuf[g, :, width // 2 :] = right
        out_copy(g).start()
        return carry

    first = min(2, steps)
    lax.fori_loop(0, first, shift_step, 0)
    pair.wait()
    total[...] = (partial[...].astype(f32) + other[...].astype(f32)).astype(bf16)
    base = me // near * near
    spot = lax.rem(me, near)
    syn_copies = []
    for d in range(1, near):
        copy = pltpu.make_async_remote_copy(
            src_ref=total, dst_ref=syn_buf.at[d], send_sem=syn_send.at[d],
            recv_sem=syn_recv.at[d], device_id={"rows": base + lax.rem(spot + d, near)},
            device_id_type=MESH,
        )
        copy.start()
        syn_copies.append(copy)
    lax.fori_loop(first, steps, shift_step, 0)

    syn_out[pl.ds(spot, 1)] = total[...][None]
    for d, copy in enumerate(syn_copies, 1):
        copy.wait()
        syn_out[pl.ds(lax.rem(spot + near - d, near), 1)] = syn_buf[d][None]
    tiles_out[pl.ds(me, 1)] = tiles_ref[...][None]
    for d, copy in enumerate(tile_copies, 1):
        copy.wait()
        tiles_out[pl.ds(lax.rem(me + count - d, count), 1)] = tile_buf[d][None]
    for g in range(steps):
        out_copy(g).wait()


def corr_kernel(
    index_ref, syn_ref, tiles_ref, colh, coll, rowh, rowl, backh, backl, lasth, lastl,
    out_ref, a_ref,
):
    syn = syn_ref[...]
    width = syn.shape[1]
    across = 2 * width // CHIP - 1
    rolled = pltpu.roll(syn.astype(f32), width - CHIP // 2, 1).astype(bf16)
    chips, tiles = [], []
    for j in range(across):
        source = rolled if j % 2 else syn
        chips.append(source[:, j // 2 * CHIP : (j // 2 + 1) * CHIP])
        tiles.append(tiles_ref[index_ref[j]])

    def spectra(blocks):
        stacked = jnp.concatenate(blocks, axis=0)
        column = dot(stacked, colh[...]) + dot(stacked, coll[...])
        for j in range(across):
            block = column[j * CHIP : (j + 1) * CHIP]
            a_ref[:CHIP, j * CHIP : (j + 1) * CHIP] = block[:, :CHIP]
            a_ref[CHIP:, j * CHIP : (j + 1) * CHIP] = block[:, CHIP:]
        return dot3((rowh[...], rowl[...]), split(a_ref[...]))

    x = spectra(chips)
    y = spectra(tiles)
    xr, xi, yr, yi = x[:CHIP], x[CHIP:], y[:CHIP], y[CHIP:]
    a_ref[:CHIP] = xr * yr + xi * yi
    a_ref[CHIP:] = xi * yr - xr * yi
    spot = index_ref[across]
    back = dot3((backh[spot], backl[spot]), split(a_ref[...]))
    height = back.shape[0] // 2
    rows = jnp.concatenate(
        [
            jnp.concatenate(
                [
                    back[:height, j * CHIP : (j + 1) * CHIP],
                    back[height:, j * CHIP : (j + 1) * CHIP],
                ],
                axis=1,
            )
            for j in range(across)
        ],
        axis=0,
    )
    surface = dot3(split(rows), (lasth[...], lastl[...]))
    for j in range(across):
        out_ref[:, j * CHIP : (j + 1) * CHIP] = surface[j * height : (j + 1) * height]


def resample_kernel(
    xs_ref, low_ref, high_ref, cos_ref, sin_ref, fe, ge, fo, go, inner_ref, rim_ref,
    out_ref, halo,
):
    width = xs_ref.shape[1]
    half = width // 2

    @pl.when(pl.program_id(0) == 0)
    def _():
        steps = halo.shape[0]
        for side, ref in enumerate((low_ref, high_ref)):
            left, right = shift_rows(ref[...], cos_ref[side], sin_ref[side], fe, ge, fo, go)
            size = ref.shape[0] // steps
            for g in range(steps):
                rows = slice(g * size, (g + 1) * size)
                halo[g, side * size : (side + 1) * size, :half] = left[rows]
                halo[g, side * size : (side + 1) * size, half:] = right[rows]

    rim = halo[pl.program_id(0)]
    size = inner_ref.shape[0]
    for s in range(GROUP // PACK):
        rows = slice(s * size, (s + 1) * size)
        out_ref[rows] = (dot(inner_ref[...], xs_ref[rows]) + dot(rim_ref[s], rim)).astype(bf16)


def keys_kernel(distance):
    magnitude = jnp.abs(distance)
    inner_part = (1.5 * magnitude - 2.5) * magnitude * magnitude + 1.0
    outer_part = ((-0.5 * magnitude + 2.5) * magnitude - 4.0) * magnitude + 2.0
    return jnp.where(magnitude <= 1.0, inner_part, jnp.where(magnitude < 2.0, outer_part, 0.0))


def offset_fields(row_offset, column_offset, across, first_row, row_count):
    chip_rows = row_offset.shape[0] // across
    scale = 64.0 * across
    row_means = jnp.sum(row_offset.astype(f32).reshape(chip_rows, across), axis=1) / scale
    column_means = jnp.sum(column_offset.astype(f32).reshape(chip_rows, across), axis=1) / scale
    centres = jnp.arange(chip_rows, dtype=f32) * CHIP + (CHIP - 1) * 0.5
    positions = first_row + jnp.arange(row_count, dtype=f32)
    clipped = jnp.clip(positions, (CHIP - 1) * 0.5, (chip_rows - 1) * CHIP + (CHIP - 1) * 0.5)
    weights = jnp.maximum(1.0 - jnp.abs(clipped[:, None] - centres[None, :]) / CHIP, 0.0)
    return (
        jnp.sum(weights * row_means[None], axis=1),
        jnp.sum(weights * column_means[None], axis=1),
    )


def on_device(
    radiance, response, reference_tiles, chip_owner, tile_slot, row_offset, column_offset,
    valid_rows,
):
    count = lax.axis_size("rows")
    device = lax.axis_index("rows")
    bands, height, width = radiance.shape
    tile_count = reference_tiles.shape[0]
    half = width // 2
    across = 2 * width // CHIP - 1
    near = CHIP // height
    first_row = device * height
    steps = bands // GROUP

    forward = [(i, i + 1) for i in range(count - 1)]
    backward = [(i + 1, i) for i in range(count - 1)]
    low = lax.ppermute(radiance[:, height - RIM :].reshape(bands * RIM, width), "rows", forward)
    high = lax.ppermute(radiance[:, :RIM].reshape(bands * RIM, width), "rows", backward)

    tables = shift_tables(width)
    columns, rows, chip_c, chip_s, last = chip_tables()

    outer = height + 2 * RIM
    row_shift, column_shift = offset_fields(
        row_offset, column_offset, across, (first_row - RIM).astype(f32), outer
    )
    numbers = first_row - RIM + jnp.arange(outer, dtype=jnp.int32)
    keep = (numbers < valid_rows[0]).astype(f32)
    frequency = np.concatenate([np.arange(0, half, 2), np.arange(1, half, 2)]).astype(np.float32)
    angles = (2.0 * math.pi / width) * frequency[None, :] * column_shift[:, None]
    turn_cos = jnp.cos(angles) * keep[:, None]
    turn_sin = jnp.sin(angles) * keep[:, None]
    own = slice(RIM, RIM + height)

    def rim_turn(turn):
        sides = jnp.stack([turn[:RIM], turn[RIM + height :]])
        return jnp.tile(sides, (1, GROUP, 1))

    keep_own = keep[own]
    shift_own = row_shift[own]

    vmem = pl.BlockSpec(memory_space=pltpu.VMEM)
    smem = pl.BlockSpec(memory_space=pltpu.SMEM)
    anywhere = pl.BlockSpec(memory_space=pl.ANY)
    dma = pltpu.SemaphoreType.DMA
    flops = 8 * bands * height * half * half
    xs, syn_all, tiles_all = pl.pallas_call(
        functools.partial(shift_kernel, near),
        out_shape=(
            jax.ShapeDtypeStruct((bands * height, width), bf16),
            jax.ShapeDtypeStruct((near, height, width), bf16),
            jax.ShapeDtypeStruct((count, tile_count, CHIP, CHIP), bf16),
        ),
        in_specs=[smem, anywhere] + [vmem] * 8,
        out_specs=(anywhere, vmem, vmem),
        scratch_shapes=[
            pltpu.VMEM((steps, GROUP, height, width), bf16),
            pltpu.VMEM((steps, GROUP * height, width), bf16),
            pltpu.VMEM((height, width), bf16),
            pltpu.VMEM((height, width), bf16),
            pltpu.VMEM((height, width), bf16),
            pltpu.VMEM((near, height, width), bf16),
            pltpu.VMEM((count, tile_count, CHIP, CHIP), bf16),
            dma((steps,)), dma((steps,)), dma((2,)),
            dma((near,)), dma((near,)), dma((count,)), dma((count,)),
        ],
        compiler_params=pltpu.CompilerParams(collective_id=0, has_side_effects=True),
        cost_estimate=pl.CostEstimate(
            flops=flops, bytes_accessed=4 * bands * height * width, transcendentals=0
        ),
        name="shift",
    )(
        response.astype(f32), radiance, reference_tiles.astype(bf16),
        jnp.broadcast_to(keep_own[:, None], (height, width)),
        turn_cos[own], turn_sin[own], *tables,
    )

    chip_row = device // near
    owner_of = lax.dynamic_slice_in_dim(chip_owner[:, 0], chip_row * across, across)
    slot_of = lax.dynamic_slice_in_dim(tile_slot, chip_row * across, across)
    index = jnp.concatenate(
        [owner_of * tile_count + slot_of, jnp.full((1,), device % near, jnp.int32)]
    )
    back = np.stack(
        [
            np.block([[chip_c[u], -chip_s[u]], [chip_s[u], chip_c[u]]])
            for u in (slice(i * height, (i + 1) * height) for i in range(near))
        ]
    )
    surface = pl.pallas_call(
        corr_kernel,
        out_shape=jax.ShapeDtypeStruct((height, across * CHIP), f32),
        in_specs=[smem] + [vmem] * 10,
        out_specs=vmem,
        scratch_shapes=[pltpu.VMEM((2 * CHIP, across * CHIP), f32)],
        cost_estimate=pl.CostEstimate(
            flops=2_500_000_000, bytes_accessed=4_000_000, transcendentals=0
        ),
        name="correlate",
    )(
        index, syn_all.reshape(near * height, width),
        tiles_all.reshape(count * tile_count, CHIP, CHIP),
        *split_np(columns), *split_np(rows), *split_np(back), *split_np(last),
    )

    size = PACK * height
    row_of = np.arange(size) % height
    band_of = np.arange(size) // height
    source = np.arange(height, dtype=np.float32)
    place = jnp.tile(source - shift_own, PACK)[:, None]
    keep_rows = jnp.tile(keep_own, PACK)[:, None]
    same = (band_of[:, None] == band_of[None, :]).astype(np.float32)
    inner = (keys_kernel(row_of[None, :].astype(np.float32) - place) * (same * keep_rows)).astype(bf16)
    rim_band = np.tile(np.repeat(np.arange(GROUP), RIM), 2)
    rim_row = np.concatenate(
        [np.tile(np.arange(RIM) - RIM, GROUP), np.tile(np.arange(RIM) + height, GROUP)]
    ).astype(np.float32)
    joined = np.stack(
        [
            (band_of[:, None] + s * PACK == rim_band[None, :]).astype(np.float32)
            for s in range(GROUP // PACK)
        ]
    )
    rim = ((keys_kernel(rim_row[None, :] - place) * keep_rows)[None] * joined).astype(bf16)

    block = pl.BlockSpec((GROUP * height, width), lambda g: (g, 0))
    aligned = pl.pallas_call(
        resample_kernel,
        grid=(steps,),
        out_shape=jax.ShapeDtypeStruct((bands * height, width), bf16),
        in_specs=[block] + [vmem] * 10,
        out_specs=block,
        scratch_shapes=[pltpu.VMEM((steps, 2 * RIM * GROUP, width), bf16)],
        compiler_params=pltpu.CompilerParams(dimension_semantics=("arbitrary",)),
        cost_estimate=pl.CostEstimate(
            flops=3_000_000_000, bytes_accessed=4 * bands * height * width, transcendentals=0
        ),
        name="resample",
    )(xs, low, high, rim_turn(turn_cos), rim_turn(turn_sin), *tables, inner, rim)
    return (aligned.reshape(bands, height, width), surface)


def solution(mesh):
    return jax.shard_map(
        on_device,
        mesh=mesh,
        in_specs=(
            P("bands", ("groups", "rows"), None),
            P("bands"),
            P(("groups", "rows"), None, None),
            P("groups", None),
            P("groups"),
            P("groups"),
            P("groups"),
            P("groups"),
        ),
        out_specs=(P("bands", ("groups", "rows"), None), P(("groups", "rows"), None)),
        check_vma=False,
    )
```

```python
import functools
import math

import jax
import jax.numpy as jnp
import numpy as np
from jax import lax
from jax.experimental import pallas as pl
from jax.experimental.pallas import tpu as pltpu
from jax.sharding import PartitionSpec as P

CHIP = 128
MAXDY = 2
RIM = MAXDY + 1
GROUP = 16
PACK = 8

MESH = pl.DeviceIdType.MESH
bf16 = jnp.bfloat16
f32 = jnp.float32


def as_bf16(a):
    return np.asarray(a, np.float32).astype(jnp.bfloat16)


def split_np(a):
    a = np.asarray(a, np.float64)
    high = as_bf16(a)
    return high, as_bf16(a - high.astype(np.float64))


def shift_tables(width):
    half = width // 2
    samples = np.arange(half)
    tables = []
    for parity in (0, 1):
        freq = np.arange(parity, half, 2)
        angle = (np.outer(samples, freq) % width) * (2.0 * np.pi / width)
        forward = np.concatenate([np.cos(angle), np.sin(angle)], axis=1)
        scale = np.where(freq == 0, 1.0, 2.0)[:, None] / width
        inverse = np.concatenate([np.cos(angle).T * scale, np.sin(angle).T * scale], axis=0)
        tables += [as_bf16(forward), as_bf16(inverse)]
    return tables


def chip_tables():
    index = np.arange(CHIP)
    angle = (np.outer(index, index) % CHIP) * (2.0 * np.pi / CHIP)
    c, s = np.cos(angle), np.sin(angle)
    window = 0.5 - 0.5 * np.cos(index * (2.0 * np.pi / CHIP))
    columns = window[:, None] * np.concatenate([c, -s], axis=1)
    cw, sw = c * window, s * window
    rows = np.block([[cw, sw], [-sw, cw]])
    last = np.concatenate([c, -s], axis=0) / float(CHIP) ** 3
    return columns, rows, c, s, last


def dot(a, b):
    return jnp.dot(a, b, preferred_element_type=f32)


def split(a):
    high = a.astype(bf16)
    return high, (a - high.astype(f32)).astype(bf16)


def dot3(a, b):
    (ah, al), (bh, bl) = a, b
    return dot(ah, bh) + dot(ah, bl) + dot(al, bh)


def keys_kernel(distance):
    magnitude = jnp.abs(distance)
    inner_part = (1.5 * magnitude - 2.5) * magnitude * magnitude + 1.0
    outer_part = ((-0.5 * magnitude + 2.5) * magnitude - 4.0) * magnitude + 2.0
    return jnp.where(magnitude <= 1.0, inner_part, jnp.where(magnitude < 2.0, outer_part, 0.0))


def field(offset_ref, numbers, across):
    chip_rows = offset_ref.shape[0] // across
    centre = (CHIP - 1) * 0.5
    clipped = jnp.clip(numbers.astype(f32), centre, (chip_rows - 1) * CHIP + centre)
    result = jnp.zeros(numbers.shape, f32)
    for k in range(chip_rows):
        total = offset_ref[k * across]
        for j in range(1, across):
            total = total + offset_ref[k * across + j]
        weight = jnp.maximum(1.0 - jnp.abs(clipped - (k * CHIP + centre)) / CHIP, 0.0)
        result = result + weight * total.astype(f32)
    return result / (64.0 * across)


def turns(column_ref, valid_ref, numbers, width, across):
    lane = lax.broadcasted_iota(jnp.int32, numbers.shape, 1)
    quarter = width // 4
    frequency = jnp.where(lane < quarter, 2 * lane, 2 * (lane - quarter) + 1).astype(f32)
    angle = (2.0 * math.pi / width) * frequency * field(column_ref, numbers, across)
    keep = jnp.where(numbers < valid_ref[0], 1.0, 0.0)
    return jnp.cos(angle) * keep, jnp.sin(angle) * keep


def shift_rows(x, cos, sin, fe, ge, fo, go):
    rows, width = x.shape
    half, quarter = width // 2, width // 4
    period = cos.shape[0]
    lo, hi = x[:, :half], x[:, half:]

    def part(values, forward, inverse, first):
        spectrum = dot(values, forward)
        turn_c = cos[:, first : first + quarter][None]
        turn_s = sin[:, first : first + quarter][None]
        c = spectrum[:, :quarter].reshape(rows // period, period, quarter)
        s = spectrum[:, quarter:].reshape(rows // period, period, quarter)
        p = (c * turn_c - s * turn_s).reshape(rows, quarter).astype(bf16)
        q = (c * turn_s + s * turn_c).reshape(rows, quarter).astype(bf16)
        return dot(p, inverse[:quarter]) + dot(q, inverse[quarter:])

    even = part(lo + hi, fe[...], ge[...], 0)
    odd = part(lo - hi, fo[...], go[...], quarter)
    return (even + odd).astype(bf16), (even - odd).astype(bf16)


def shift_kernel(
    near,
    resp_ref, column_ref, valid_ref, x_hbm, tiles_ref, fe, ge, fo, go,
    xs_hbm, syn_out, tiles_out,
    own_tiles, cos_ref, sin_ref, xbuf, obuf, partial, other, total, syn_buf, tile_buf,
    in_sem, out_sem, pair_sem, syn_send, syn_recv, tile_send, tile_recv,
):
    count = lax.axis_size("rows")
    me = lax.axis_index("rows")
    core = lax.axis_index("bands")
    steps, group, height, width = xbuf.shape
    in_copies = [
        pltpu.make_async_copy(x_hbm.at[pl.ds(g * group, group)], xbuf.at[g], in_sem.at[g])
        for g in range(steps)
    ]
    for copy in in_copies:
        copy.start()

    own_tiles[...] = tiles_ref[...].astype(bf16)
    barrier = pltpu.get_barrier_semaphore()
    for d in range(1, count):
        pl.semaphore_signal(
            barrier, inc=1, device_id={"rows": lax.rem(me + d, count)}, device_id_type=MESH
        )
    pl.semaphore_signal(barrier, inc=1, device_id={"bands": 1 - core}, device_id_type=MESH)
    pl.semaphore_wait(barrier, count)

    tile_copies = []
    for d in range(1, count):
        copy = pltpu.make_async_remote_copy(
            src_ref=own_tiles, dst_ref=tile_buf.at[d], send_sem=tile_send.at[d],
            recv_sem=tile_recv.at[d], device_id={"rows": lax.rem(me + d, count)},
            device_id_type=MESH,
        )
        copy.start()
        tile_copies.append(copy)

    across = 2 * width // CHIP - 1
    numbers = me * height + lax.broadcasted_iota(jnp.int32, cos_ref.shape, 0)
    cos_ref[...], sin_ref[...] = turns(column_ref, valid_ref, numbers, width, across)
    acc = jnp.zeros((height, width), f32)
    for g in range(steps):
        in_copies[g].wait()

        def add(b, acc, g=g):
            return acc + resp_ref[g * group + b] * xbuf[g, b].astype(f32)

        acc = lax.fori_loop(0, group, add, acc)
    numbers = me * height + lax.broadcasted_iota(jnp.int32, acc.shape, 0)
    partial[...] = jnp.where(numbers < valid_ref[0], acc, 0.0).astype(bf16)
    pair = pltpu.make_async_remote_copy(
        src_ref=partial, dst_ref=other, send_sem=pair_sem.at[0], recv_sem=pair_sem.at[1],
        device_id={"bands": 1 - core}, device_id_type=MESH,
    )
    pair.start()

    def out_copy(g):
        return pltpu.make_async_copy(
            obuf.at[g], xs_hbm.at[pl.ds(g * group * height, group * height)], out_sem.at[g]
        )

    def shift_step(g, carry):
        x = xbuf[g].reshape(group * height, width)
        left, right = shift_rows(x, cos_ref[...], sin_ref[...], fe, ge, fo, go)
        obuf[g, :, : width // 2] = left
        obuf[g, :, width // 2 :] = right
        out_copy(g).start()
        return carry

    first = min(2, steps)
    lax.fori_loop(0, first, shift_step, 0)
    pair.wait()
    total[...] = (partial[...].astype(f32) + other[...].astype(f32)).astype(bf16)
    base = me // near * near
    spot = lax.rem(me, near)
    syn_copies = []
    for d in range(1, near):
        copy = pltpu.make_async_remote_copy(
            src_ref=total, dst_ref=syn_buf.at[d], send_sem=syn_send.at[d],
            recv_sem=syn_recv.at[d], device_id={"rows": base + lax.rem(spot + d, near)},
            device_id_type=MESH,
        )
        copy.start()
        syn_copies.append(copy)
    lax.fori_loop(first, steps, shift_step, 0)

    syn_out[pl.ds(spot, 1)] = total[...][None]
    for d, copy in enumerate(syn_copies, 1):
        copy.wait()
        syn_out[pl.ds(lax.rem(spot + near - d, near), 1)] = syn_buf[d][None]
    tiles_out[pl.ds(me, 1)] = own_tiles[...][None]
    for d, copy in enumerate(tile_copies, 1):
        copy.wait()
        tiles_out[pl.ds(lax.rem(me + count - d, count), 1)] = tile_buf[d][None]
    for g in range(steps):
        out_copy(g).wait()


def corr_kernel(
    near, held, owner_ref, slot_ref, device_ref, syn_ref, tiles_ref, colh, coll, rowh, rowl, backh, backl, lasth, lastl,
    out_ref, a_ref,
):
    syn = syn_ref[...]
    width = syn.shape[1]
    across = 2 * width // CHIP - 1
    rolled = pltpu.roll(syn.astype(f32), width - CHIP // 2, 1).astype(bf16)
    first = device_ref[0] // near * across
    chips, tiles = [], []
    for j in range(across):
        source = rolled if j % 2 else syn
        chips.append(source[:, j // 2 * CHIP : (j // 2 + 1) * CHIP])
        tiles.append(tiles_ref[owner_ref[first + j] * held + slot_ref[first + j]])

    def spectra(blocks):
        stacked = jnp.concatenate(blocks, axis=0)
        column = dot(stacked, colh[...]) + dot(stacked, coll[...])
        for j in range(across):
            block = column[j * CHIP : (j + 1) * CHIP]
            a_ref[:CHIP, j * CHIP : (j + 1) * CHIP] = block[:, :CHIP]
            a_ref[CHIP:, j * CHIP : (j + 1) * CHIP] = block[:, CHIP:]
        return dot3((rowh[...], rowl[...]), split(a_ref[...]))

    x = spectra(chips)
    y = spectra(tiles)
    xr, xi, yr, yi = x[:CHIP], x[CHIP:], y[:CHIP], y[CHIP:]
    a_ref[:CHIP] = xr * yr + xi * yi
    a_ref[CHIP:] = xi * yr - xr * yi
    spot = lax.rem(device_ref[0], near)
    back = dot3((backh[spot], backl[spot]), split(a_ref[...]))
    height = back.shape[0] // 2
    rows = jnp.concatenate(
        [
            jnp.concatenate(
                [
                    back[:height, j * CHIP : (j + 1) * CHIP],
                    back[height:, j * CHIP : (j + 1) * CHIP],
                ],
                axis=1,
            )
            for j in range(across)
        ],
        axis=0,
    )
    surface = dot3(split(rows), (lasth[...], lastl[...]))
    for j in range(across):
        out_ref[:, j * CHIP : (j + 1) * CHIP] = surface[j * height : (j + 1) * height]


def resample_kernel(
    height, row_ref, column_ref, valid_ref, device_ref, xs_ref, low_ref, high_ref,
    fe, ge, fo, go, out_ref, halo, inner_ref, rim_ref,
):
    width = xs_ref.shape[1]
    half = width // 2
    across = 2 * width // CHIP - 1
    size = PACK * height

    @pl.when(pl.program_id(0) == 0)
    def _():
        first_row = device_ref[0] * height
        steps = halo.shape[0]
        bands = steps * GROUP
        for side, ref in enumerate((low_ref, high_ref)):
            start = first_row + (height if side else -RIM)
            numbers = start + lax.broadcasted_iota(jnp.int32, (8, half), 0)
            cos, sin = turns(column_ref, valid_ref, numbers, width, across)
            for j in range(RIM):
                left, right = shift_rows(
                    ref[j * bands : (j + 1) * bands], cos[j : j + 1], sin[j : j + 1],
                    fe, ge, fo, go,
                )
                place = (side * RIM + j) * GROUP
                for g in range(steps):
                    rows = slice(g * GROUP, (g + 1) * GROUP)
                    halo[g, place : place + GROUP, :half] = left[rows]
                    halo[g, place : place + GROUP, half:] = right[rows]

        def matrix(columns, target, joined):
            spread = lax.broadcasted_iota(jnp.int32, (size, columns), 0)
            row = spread & (height - 1)
            band = spread // height
            column = lax.broadcasted_iota(jnp.int32, (size, columns), 1)
            numbers = first_row + row
            source = row.astype(f32) - field(row_ref, numbers, across)
            value = keys_kernel(target(column).astype(f32) - source)
            used = joined(column, band) & (numbers < valid_ref[0])
            return jnp.where(used, value, 0.0).astype(bf16)

        inner_ref[...] = matrix(
            size, lambda c: c & (height - 1), lambda c, band: c // height == band
        )

        def rim_target(c):
            line = c // GROUP
            return jnp.where(line < RIM, line - RIM, line - RIM + height)

        for s in range(GROUP // PACK):
            rim_ref[s] = matrix(
                2 * RIM * GROUP, rim_target,
                lambda c, band, s=s: (c & (GROUP - 1)) == band + s * PACK,
            )

    rim = halo[pl.program_id(0)]
    for s in range(GROUP // PACK):
        rows = slice(s * size, (s + 1) * size)
        out_ref[rows] = (dot(inner_ref[...], xs_ref[rows]) + dot(rim_ref[s], rim)).astype(bf16)


def on_device(
    radiance, response, reference_tiles, chip_owner, tile_slot, row_offset, column_offset,
    valid_rows,
):
    count = lax.axis_size("rows")
    device = lax.axis_index("rows")
    bands, height, width = radiance.shape
    tile_count = reference_tiles.shape[0]
    half = width // 2
    across = 2 * width // CHIP - 1
    near = CHIP // height
    first_row = device * height
    steps = bands // GROUP

    forward = [(i, i + 1) for i in range(count - 1)]
    backward = [(i + 1, i) for i in range(count - 1)]
    low = lax.ppermute(radiance[:, height - RIM :].transpose(1, 0, 2).reshape(bands * RIM, width), "rows", forward)
    high = lax.ppermute(radiance[:, :RIM].transpose(1, 0, 2).reshape(bands * RIM, width), "rows", backward)

    tables = shift_tables(width)
    columns, rows, chip_c, chip_s, last = chip_tables()

    where = jnp.full((1,), device, jnp.int32)
    vmem = pl.BlockSpec(memory_space=pltpu.VMEM)
    smem = pl.BlockSpec(memory_space=pltpu.SMEM)
    anywhere = pl.BlockSpec(memory_space=pl.ANY)
    dma = pltpu.SemaphoreType.DMA
    flops = 8 * bands * height * half * half
    xs, syn_all, tiles_all = pl.pallas_call(
        functools.partial(shift_kernel, near),
        out_shape=(
            jax.ShapeDtypeStruct((bands * height, width), bf16),
            jax.ShapeDtypeStruct((near, height, width), bf16),
            jax.ShapeDtypeStruct((count, tile_count, CHIP, CHIP), bf16),
        ),
        in_specs=[smem] * 3 + [anywhere] + [vmem] * 5,
        out_specs=(anywhere, vmem, vmem),
        scratch_shapes=[
            pltpu.VMEM((tile_count, CHIP, CHIP), bf16),
            pltpu.VMEM((height, half), f32),
            pltpu.VMEM((height, half), f32),
            pltpu.VMEM((steps, GROUP, height, width), bf16),
            pltpu.VMEM((steps, GROUP * height, width), bf16),
            pltpu.VMEM((height, width), bf16),
            pltpu.VMEM((height, width), bf16),
            pltpu.VMEM((height, width), bf16),
            pltpu.VMEM((near, height, width), bf16),
            pltpu.VMEM((count, tile_count, CHIP, CHIP), bf16),
            dma((steps,)), dma((steps,)), dma((2,)),
            dma((near,)), dma((near,)), dma((count,)), dma((count,)),
        ],
        compiler_params=pltpu.CompilerParams(collective_id=0, has_side_effects=True),
        cost_estimate=pl.CostEstimate(
            flops=flops, bytes_accessed=4 * bands * height * width, transcendentals=0
        ),
        name="shift",
    )(
        response.astype(f32), column_offset, valid_rows, radiance, reference_tiles, *tables,
    )

    back = np.stack(
        [
            np.block([[chip_c[u], -chip_s[u]], [chip_s[u], chip_c[u]]])
            for u in (slice(i * height, (i + 1) * height) for i in range(near))
        ]
    )
    surface = pl.pallas_call(
        functools.partial(corr_kernel, near, tile_count),
        out_shape=jax.ShapeDtypeStruct((height, across * CHIP), f32),
        in_specs=[smem] * 3 + [vmem] * 10,
        out_specs=vmem,
        scratch_shapes=[pltpu.VMEM((2 * CHIP, across * CHIP), f32)],
        cost_estimate=pl.CostEstimate(
            flops=2_500_000_000, bytes_accessed=4_000_000, transcendentals=0
        ),
        name="correlate",
    )(
        chip_owner[:, 0], tile_slot, where, syn_all.reshape(near * height, width),
        tiles_all.reshape(count * tile_count, CHIP, CHIP),
        *split_np(columns), *split_np(rows), *split_np(back), *split_np(last),
    )

    block = pl.BlockSpec((GROUP * height, width), lambda g: (g, 0))
    aligned = pl.pallas_call(
        functools.partial(resample_kernel, height),
        grid=(steps,),
        out_shape=jax.ShapeDtypeStruct((bands * height, width), bf16),
        in_specs=[smem] * 4 + [block] + [vmem] * 6,
        out_specs=block,
        scratch_shapes=[
            pltpu.VMEM((steps, 2 * RIM * GROUP, width), bf16),
            pltpu.VMEM((PACK * height, PACK * height), bf16),
            pltpu.VMEM((GROUP // PACK, PACK * height, 2 * RIM * GROUP), bf16),
        ],
        compiler_params=pltpu.CompilerParams(dimension_semantics=("arbitrary",)),
        cost_estimate=pl.CostEstimate(
            flops=3_000_000_000, bytes_accessed=4 * bands * height * width, transcendentals=0
        ),
        name="resample",
    )(row_offset, column_offset, valid_rows, where, xs, low, high, *tables)
    return (aligned.reshape(bands, height, width), surface)


def solution(mesh):
    return jax.shard_map(
        on_device,
        mesh=mesh,
        in_specs=(
            P("bands", ("groups", "rows"), None),
            P("bands"),
            P(("groups", "rows"), None, None),
            P("groups", None),
            P("groups"),
            P("groups"),
            P("groups"),
            P("groups"),
        ),
        out_specs=(P("bands", ("groups", "rows"), None), P(("groups", "rows"), None)),
        check_vma=False,
    )
```
